32 devices in a mesh: ctx: 8 (over y, x, core), exp: 4 (over z).
Axes of the slice: x: 2, y: 2, z: 4, core: 2. Of those that a mesh axis runs over, the one named last changes fastest.
Arguments:
- resid: bfloat16 [1024, 6400], P('ctx', 'exp'), may hold values from -6 to 6
- ssm_input: bfloat16 [1024, 6400], P('ctx', 'exp'), may hold values from -0.1875 to 0.1875
- bc_proj: bfloat16 [1024, 1024], P('ctx', 'exp'), may hold values from -1.75 to 1.75
- log_decay: float32 [100, 1024], P('exp', 'ctx'), may hold values from -0.8 to 0
- experts_idx: int32 [1024, 2], P('ctx'), may hold values from 0 to 7, all different within a row; in each aligned block of 128 rows (0 to 127, 128 to 255, ...) at most 48 rows name the same one
- route_weight: float32 [1024, 2], P('ctx'), may hold values from 0.1 to 0.9
- w_gate: bfloat16 [8, 6400, 1024], P('ctx', 'exp'), may hold values from -0.078125 to 0.078125
- w_up: bfloat16 [8, 6400, 1024], P('ctx', 'exp'), may hold values from -0.078125 to 0.078125
- w_down: bfloat16 [8, 1024, 6400], P('ctx', None, 'exp'), may hold values from -0.1875 to 0.1875
- cotangent: bfloat16 [1024, 6400], P('ctx', 'exp'), may hold values from -6 to 6
Outputs:
- final: bfloat16 [1024, 6400], P('ctx', 'exp')
- d_resid: bfloat16 [1024, 6400], P('ctx', 'exp')
- d_input: bfloat16 [1024, 6400], P('ctx', 'exp')
- d_proj: bfloat16 [1024, 1024], P('ctx', 'exp')
- d_decay: float32 [100, 1024], P('exp', 'ctx')
The draws below stay inside these ranges and needn't reach their ends.
Inputs may be any that keep to these rules, and one draw needn't show every extreme that they name: `experts_idx`: each row names two different experts; within the rows of one index of ctx no expert is named more than 48 times, and in some such rows one expert is named exactly 48 times.
All inputs are finite; a program needn't handle non-finite values.
Results may differ from the reference program's by a relative error of at most 0.019.
Values may be sent and summed in bfloat16 or wider, within the bound.
No kernel may reach another device: no remote copies, remote signals or barrier semaphores. Data moves between devices by JAX's collectives and lax.ppermute only.
A program may use at most 192 MiB of HBM per device.

```python
import math
import jax
import jax.numpy as jnp
import numpy as np
from jax import lax

D = 6400
BLENDER_LANES = 100
STATE = 128
GROUPS = 4
FF = 1024
EXPERTS = 8
TOK_DEV = 128
STRING_LENGTH = 1024
CAPE = 48
N_CTX = 8
N_EXP = 4


def draw_log_decay(key, part):
    concurrent_currents = jax.random.split(key, 7)
    quick_share = 0.5
    quick_heads = jax.random.uniform(concurrent_currents[0], (BLENDER_LANES, 1)) < quick_share
    quick_rate = jnp.exp(jax.random.uniform(concurrent_currents[1], (BLENDER_LANES, 1), minval=math.log(1.0 / 50.0), maxval=math.log(1.0 / 30.0)))
    slow_rate = jnp.exp(jax.random.uniform(concurrent_currents[2], (BLENDER_LANES, 1), minval=math.log(0.1), maxval=math.log(0.6))) / STRING_LENGTH
    fading_rate = jnp.where(quick_heads, quick_rate, slow_rate)
    blocks = STRING_LENGTH // TOK_DEV
    machine_factor = jnp.exp(jax.random.uniform(concurrent_currents[3], (BLENDER_LANES, blocks, 1), minval=math.log(0.6), maxval=math.log(1.6)))
    machine_factor = jnp.broadcast_to(machine_factor, (BLENDER_LANES, blocks, TOK_DEV)).reshape(BLENDER_LANES, STRING_LENGTH)
    stochastic_jitter = jax.random.uniform(concurrent_currents[4], (BLENDER_LANES, STRING_LENGTH), minval=0.5, maxval=1.5)
    spike_tallies = jax.random.uniform(concurrent_currents[5], (BLENDER_LANES, STRING_LENGTH)) < 2.0 / STRING_LENGTH
    grand_quantity = jnp.log(jax.random.uniform(concurrent_currents[6], (BLENDER_LANES, STRING_LENGTH), minval=0.5, maxval=0.8))
    return jnp.where(spike_tallies, grand_quantity, 0.0) - fading_rate * machine_factor * stochastic_jitter


def block_levels(stream_key, dims, cuts, smallest, largest):
    gain = 1.0
    for dim, shards_of in cuts:
        draws = jax.random.uniform(jax.random.fold_in(jax.random.fold_in(stream_key, 6), dim), (shards_of,), jnp.float32, smallest / len(cuts), largest / len(cuts))
        gain = gain * jnp.repeat(jnp.exp(draws), dims[dim] // shards_of).reshape((-1,) + (1,) * (len(dims) - 1 - dim))
    return gain


def routed_block(rng, own, number, rows, number_of, top, limit, skew):
    order = jax.random.permutation(rng, number_of)
    packed, usual = load_shares(number_of, rows * top, limit, skew, True), load_shares(number_of, rows * top, limit, skew, False)
    places = jnp.arange(number_of)

    def named(sizes, offset_by):
        used = int((sizes > 0).sum())
        fixed = max(1, used // 4)
        passed = fixed + (places - fixed + offset_by * (used - fixed)) % max(1, number_of - fixed)
        return jnp.zeros((number_of,), jnp.int32).at[order[jnp.where(places < fixed, places, passed)]].set(jnp.asarray(sizes, jnp.int32))

    sizes = jnp.where(number % 4 == 0, named(packed, number // 4), named(usual, number - number // 4 - 1))
    mixed = jax.random.permutation(jax.random.fold_in(own, 3), number_of)
    giver, sink = mixed[0:number_of // 2 * 2:2], mixed[1:number_of // 2 * 2:2]
    margin = jnp.minimum(sizes[giver] - 1, limit - sizes[sink]) // 2
    margin = jnp.where((giver == order[0]) | (sink == order[0]) | (sizes[sink] == 0), 0, jnp.maximum(margin, 0))
    passed = jax.random.randint(jax.random.fold_in(own, 4), (number_of // 2,), 0, 1 << 20) % (margin + 1)
    sizes = sizes.at[giver].add(-passed).at[sink].add(passed)
    members = jnp.searchsorted(jnp.cumsum(sizes), jnp.arange(rows * top), side="right").astype(jnp.int32)
    grid = members.reshape(top, rows).T
    grid = grid[jax.random.permutation(jax.random.fold_in(own, 1), rows)]
    offset_by = jax.random.randint(jax.random.fold_in(own, 2), (rows, 1), 0, top)
    return jnp.take_along_axis(grid, (jnp.arange(top)[None, :] + offset_by) % top, axis=1)


def load_shares(amount, total, most, skew, full):
    loads = [(1 << 20) // math.isqrt(standing ** skew) + 1 for standing in range(1, amount + 1)]
    largest = most if full else min(most, max(-(-total // amount), total * loads[0] // sum(loads)))
    least = 1 if total - largest >= amount - 1 else 0
    given, surplus = [largest] + [least] * (amount - 1), total - largest - least * (amount - 1)
    while surplus > 0:
        free = [i for i in range(1, amount) if given[i] < largest] or [i for i in range(1, amount) if given[i] < most]
        whole, budget = sum([loads[i] for i in free]), surplus
        for i in free:
            more = min(most - given[i], max(1, budget * loads[i] // whole), surplus)
            given[i] = given[i] + more
            surplus = surplus - more
    return np.array(given)


def scatter_about(rng, dims, scale, reach, shards=(), dtype=jnp.bfloat16):
    values = jax.random.normal(rng, dims, jnp.float32) * scale
    if len(shards) > 0:
        values = block_levels(rng, dims, shards, -0.22, 0.18) * values
    return jnp.clip(values, min=-reach, max=reach).astype(dtype)


def setup_inputs(seed: int = 0) -> dict:
    key_list = jax.random.split(jax.random.key(seed), 11)
    resid = scatter_about(key_list[0], (STRING_LENGTH, D), 1.0, 6.0, ((0, 8), (1, 4)))
    ssm_input = scatter_about(key_list[1], (STRING_LENGTH, D), 0.03, 0.1875, ((0, 8), (1, 4)))
    bc_proj = scatter_about(key_list[2], (STRING_LENGTH, 2 * GROUPS * STATE), 0.3, 1.75, ((0, 8), (1, 4)))
    log_decay = draw_log_decay(jax.random.fold_in(key_list[10], 71), 0)
    experts_idx_keys = jax.random.split(jax.random.fold_in(key_list[4], 1), STRING_LENGTH // TOK_DEV)
    experts_idx_turns = jax.random.permutation(jax.random.fold_in(key_list[4], 3), STRING_LENGTH // TOK_DEV)
    experts_idx = jax.vmap(lambda own, number: routed_block(jax.random.fold_in(key_list[4], 2), own, number, TOK_DEV, EXPERTS, 2, CAPE, 2))(experts_idx_keys, experts_idx_turns).reshape((STRING_LENGTH, 2))
    route_weight = jnp.clip(0.1 + 0.79999997 * jax.random.uniform(key_list[5], (STRING_LENGTH, 2), jnp.float32) ** block_levels(key_list[5], (STRING_LENGTH, 2), ((0, 8),), -0.2, 0.2), 0.1, 0.9)
    w_gate = scatter_about(key_list[6], (EXPERTS, D, FF), D ** -0.5, 0.078125, ((0, 8), (1, 4)))
    w_up = scatter_about(key_list[7], (EXPERTS, D, FF), D ** -0.5, 0.078125, ((0, 8), (1, 4)))
    w_down = scatter_about(key_list[8], (EXPERTS, FF, D), FF ** -0.5, 0.1875, ((0, 8), (2, 4)))
    cotangent = scatter_about(key_list[9], (STRING_LENGTH, D), 1.0, 6.0, ((0, 8), (1, 4)))
    return dict(resid=resid, ssm_input=ssm_input, bc_proj=bc_proj, log_decay=log_decay, experts_idx=experts_idx, route_weight=route_weight, w_gate=w_gate, w_up=w_up, w_down=w_down, cotangent=cotangent)


highest = lax.Precision.HIGHEST

def local_terms(inputs, projection, decay_rows):
    steps_count, feature_width = inputs.shape
    heads_count = decay_rows.shape[0]
    head_width = feature_width // heads_count
    state_width = projection.shape[1] // 2
    b_part = projection[:, :state_width]
    c_part = projection[:, state_width:]
    cumulative = jnp.cumsum(decay_rows, axis=1)
    causal = jnp.arange(steps_count)[:, None] >= jnp.arange(steps_count)[None, :]
    spread = cumulative[:, :, None] - cumulative[:, None, :]
    kernel = jnp.where(causal[None], jnp.exp(jnp.where(causal[None], spread, 0.0)), 0.0)
    inner_cb = jnp.dot(c_part, b_part.T, precision=highest)
    shaped = inputs.reshape(steps_count, heads_count, head_width)
    intra_part = jnp.einsum('hts,shp->thp', kernel * inner_cb[None], shaped, precision=highest).reshape(steps_count, feature_width)
    tail_scale = jnp.exp(cumulative[:, -1:] - cumulative)
    weighted = (shaped * tail_scale.T[:, :, None]).reshape(steps_count, feature_width)
    state_local = jnp.dot(b_part.T, weighted, precision=highest)
    carry_scale = jnp.repeat(jnp.exp(cumulative[:, -1]), head_width)
    return (intra_part, state_local, carry_scale, cumulative)

def carried_terms(projection, cumulative, state_in):
    state_width = projection.shape[1] // 2
    head_width = state_in.shape[1] // cumulative.shape[0]
    from_state = jnp.dot(projection[:, state_width:], state_in, precision=highest)
    return from_state * jnp.repeat(jnp.exp(cumulative).T, head_width, axis=1)

def ssd_block(inputs, projection, decay_rows, state_in):
    intra_part, state_local, carry_scale, cumulative = local_terms(inputs, projection, decay_rows)
    output = intra_part + carried_terms(projection, cumulative, state_in)
    return (output, carry_scale[None, :] * state_in + state_local)

def silu_parts(gate_sum):
    sigmoid_part = jax.nn.sigmoid(gate_sum)
    return (gate_sum * sigmoid_part, sigmoid_part * (1.0 + gate_sum * (1.0 - sigmoid_part)))

def hidden_section(gate_sum, up_sum, back_sum):
    active, slope_part = silu_parts(gate_sum)
    hidden = (active * up_sum).astype(jnp.bfloat16)
    grad_gate = (back_sum * up_sum * slope_part).astype(jnp.bfloat16)
    grad_up = (back_sum * active).astype(jnp.bfloat16)
    return (hidden, grad_gate, grad_up)

def settle(value):
    return lax.optimization_barrier(value.astype(jnp.bfloat16)).astype(jnp.float32)

def expert_block(rows_mixed, rows_cot, gate_w, up_w, down_w):
    block_width = rows_mixed.shape[1] // N_EXP
    hidden_width = gate_w.shape[1]
    gate_sum = jnp.zeros((rows_mixed.shape[0], hidden_width), jnp.float32)
    up_sum = jnp.zeros((rows_mixed.shape[0], hidden_width), jnp.float32)
    back_sum = jnp.zeros((rows_mixed.shape[0], hidden_width), jnp.float32)
    for part_index in range(N_EXP):
        column_block = slice(part_index * block_width, (part_index + 1) * block_width)
        gate_sum = gate_sum + settle(jnp.dot(rows_mixed[:, column_block], gate_w[column_block], preferred_element_type=jnp.float32))
        up_sum = up_sum + settle(jnp.dot(rows_mixed[:, column_block], up_w[column_block], preferred_element_type=jnp.float32))
        back_sum = back_sum + settle(jnp.dot(rows_cot[:, column_block], down_w[:, column_block].T, preferred_element_type=jnp.float32))
    hidden, grad_gate, grad_up = hidden_section(gate_sum, up_sum, back_sum)
    expert_out = jnp.dot(hidden, down_w, preferred_element_type=jnp.float32).astype(jnp.bfloat16)
    expert_back = (jnp.dot(grad_gate, gate_w.T, preferred_element_type=jnp.float32) + jnp.dot(grad_up, up_w.T, preferred_element_type=jnp.float32)).astype(jnp.bfloat16)
    return (expert_out, expert_back)

def reference(resid, ssm_input, bc_proj, log_decay, experts_idx, route_weight, w_gate, w_up, w_down, cotangent):
    tokens_count, feature_width = resid.shape
    heads_count = log_decay.shape[0]
    group_width = feature_width // GROUPS
    group_heads = heads_count // GROUPS
    state_width = bc_proj.shape[1] // (2 * GROUPS)

    def mixer(inputs, projection, decay_rows):
        pieces_out = []
        for group_index in range(GROUPS):
            inputs_group = inputs[:, group_index * group_width:(group_index + 1) * group_width].reshape(N_CTX, TOK_DEV, group_width)
            proj_group = projection[:, group_index * 2 * state_width:(group_index + 1) * 2 * state_width].reshape(N_CTX, TOK_DEV, 2 * state_width)
            decay_group = decay_rows[group_index * group_heads:(group_index + 1) * group_heads].reshape(group_heads, N_CTX, TOK_DEV).transpose(1, 0, 2)

            def stepper(state_now, pieces):
                output, state_next = ssd_block(pieces[0], pieces[1], pieces[2], state_now)
                return (state_next, output)
            _, outputs = lax.scan(stepper, jnp.zeros((state_width, group_width), jnp.float32), (inputs_group, proj_group, decay_group))
            pieces_out.append(outputs.reshape(tokens_count, group_width))
        return jnp.concatenate(pieces_out, axis=1)
    mixer_out, mixer_back = jax.vjp(mixer, ssm_input.astype(jnp.float32), bc_proj.astype(jnp.float32), log_decay)
    mixed_rows = (resid.astype(jnp.float32) + mixer_out).astype(jnp.bfloat16)
    chosen = experts_idx.reshape(-1)
    assign_count = chosen.shape[0]
    token_of = (jnp.arange(assign_count) // 2).astype(jnp.int32)
    expert_count = w_gate.shape[0]
    onehot = (chosen[:, None] == jnp.arange(expert_count)[None, :]).astype(jnp.int32)
    slot_rank = (lax.optimization_barrier(jnp.sum(jnp.cumsum(onehot, axis=0) * onehot, axis=1)) - 1).astype(jnp.int32)
    rows_cap = N_CTX * CAPE
    slot_table = jnp.full((expert_count, rows_cap), tokens_count, jnp.int32).at[chosen, slot_rank].set(token_of)
    mixed_pad = jnp.concatenate([mixed_rows, jnp.zeros((1, feature_width), jnp.bfloat16)], axis=0)
    cot_pad = jnp.concatenate([cotangent, jnp.zeros((1, feature_width), jnp.bfloat16)], axis=0)

    def per_expert(pieces):
        slot_rows, gate_w, up_w, down_w = pieces
        return expert_block(mixed_pad[slot_rows], cot_pad[slot_rows], gate_w, up_w, down_w)
    expert_outs, expert_backs = lax.map(per_expert, (slot_table, w_gate, w_up, w_down))
    picked_out = expert_outs[chosen, slot_rank].reshape(tokens_count, 2, feature_width)
    picked_back = expert_backs[chosen, slot_rank].reshape(tokens_count, 2, feature_width)
    expert_mix = lax.optimization_barrier(jnp.sum(picked_out.astype(jnp.float32) * route_weight[:, :, None], axis=1))
    final_rows = (mixed_rows.astype(jnp.float32) + expert_mix).astype(jnp.bfloat16)
    grad_mixed = cotangent.astype(jnp.float32) + lax.optimization_barrier(jnp.sum(picked_back.astype(jnp.float32) * route_weight[:, :, None], axis=1))
    grad_inputs, grad_proj, grad_decay = mixer_back(grad_mixed)
    return (final_rows, grad_mixed.astype(jnp.bfloat16), grad_inputs.astype(jnp.bfloat16), grad_proj.astype(jnp.bfloat16), grad_decay)
```

```python
import functools

import jax
import jax.numpy as jnp
import numpy as np
from jax import lax
from jax.experimental import pallas as pl
from jax.experimental.pallas import tpu as pltpu
from jax.sharding import PartitionSpec as P


f32, bf16 = jnp.float32, jnp.bfloat16
exact = lax.Precision.HIGHEST
PAD = 16


def nt(a, b):
    return lax.dot_general(a, b, (((1,), (1,)), ((), ())), preferred_element_type=f32)


def tn(a, b):
    return lax.dot_general(a, b, (((0,), (0,)), ((), ())), preferred_element_type=f32)


def nn(a, b):
    return lax.dot_general(a, b, (((1,), (0,)), ((), ())), preferred_element_type=f32)


def iota(shape, dim):
    return lax.broadcasted_iota(jnp.int32, shape, dim)


def split2(v):
    high = v.astype(bf16)
    return high, (v - high.astype(f32)).astype(bf16)


def split3(v):
    high, rest = v.astype(bf16), None
    rest = v - high.astype(f32)
    mid = rest.astype(bf16)
    return high, mid, (rest - mid.astype(f32)).astype(bf16)


def call(body, outs, *args, smem=0, scratch=(), cost=None):
    specs = [pl.BlockSpec(memory_space=pltpu.SMEM)] * smem
    specs += [pl.BlockSpec(memory_space=pltpu.VMEM)] * (len(args) - smem)
    moved = sum(int(np.prod(a.shape)) * a.dtype.itemsize for a in list(args) + list(outs))
    flops = cost or 4 * moved
    return pl.pallas_call(
        body,
        out_shape=outs,
        in_specs=specs,
        out_specs=[pl.BlockSpec(memory_space=pltpu.VMEM)] * len(outs),
        scratch_shapes=list(scratch),
        cost_estimate=pl.CostEstimate(flops=flops, bytes_accessed=moved, transcendentals=0),
    )(*args)


def struct(shape, dtype):
    return jax.ShapeDtypeStruct(tuple(shape), dtype)


def route_body(me, idx, weight, block, rank_of, rows, sel, sel_hi, sel_lo, sent):
    tokens, slots = idx.shape[0], block.shape[0]
    lanes = 128
    expert = iota((tokens, lanes), 1)
    first, second = idx[:, 0:1] == expert, idx[:, 1:2] == expert
    named = first | second
    earlier = (iota((tokens, tokens), 1) < iota((tokens, tokens), 0)).astype(f32).astype(bf16)
    rank = nn(earlier, named.astype(f32).astype(bf16))
    value = jnp.where(named, rank, -1.0).astype(bf16)
    of_slot = ((block[...] ^ me[0]) == iota((slots, lanes), 1)).astype(f32).astype(bf16)
    chosen = nt(of_slot, value) == rank_of[...]
    weights = jnp.where(first, weight[:, 0:1], 0.0) + jnp.where(second, weight[:, 1:2], 0.0)
    high, low = split2(weights)
    picks = chosen.astype(f32).astype(bf16)
    sel[...] = picks
    sel_hi[...] = jnp.where(chosen, nt(of_slot, high), 0.0).astype(bf16)
    sel_lo[...] = jnp.where(chosen, nt(of_slot, low), 0.0).astype(bf16)
    sent[...] = nn(picks, rows[...]).astype(bf16)


def spans(heads, width):
    size = width // heads
    return [
        (h * size, min(h + 2, heads) * size, h, min(h + 1, heads - 1), size)
        for h in range(0, heads, 2)
    ]


def by_head(table, span, rows=slice(None)):
    begin, end, h0, h1, size = span
    left = table[rows, h0 : h0 + 1]
    if h0 == h1:
        return jnp.broadcast_to(left, (left.shape[0], end - begin))
    right = table[rows, h1 : h1 + 1]
    return jnp.where(iota((left.shape[0], end - begin), 1) < size, left, right)


def forward_body(inputs, proj, decay, intra, pay, cum_out, cum_t_out):
    tokens, width = inputs.shape
    heads, state = decay.shape[0], proj.shape[1] // 2
    rows, cols = iota((tokens, tokens), 0), iota((tokens, tokens), 1)
    upper, lower = (rows <= cols).astype(f32), (rows >= cols).astype(f32)
    cum = lax.dot_general(
        decay[...], upper, (((1,), (0,)), ((), ())), precision=exact, preferred_element_type=f32
    )
    cum_t = lax.dot_general(
        lower, decay[...], (((1,), (1,)), ((), ())), precision=exact, preferred_element_type=f32
    )
    cum_out[...] = cum
    cum_t_out[...] = cum_t
    b_part, c_part = proj[:, :state], proj[:, state:]
    inner = nt(c_part, b_part)
    causal = rows >= cols
    tail = jnp.exp(cum_t[tokens - 1 : tokens, :] - cum_t)
    carry = jnp.exp(cum_t[tokens - 1 : tokens, :])
    place = iota((PAD, 2 * (width // heads)), 0)
    for span in spans(heads, width):
        begin, end, h0, h1, size = span
        x = inputs[:, begin:end]
        parts = []
        for h in (h0, h1)[: 1 + (h1 > h0)]:
            spread = jnp.where(causal, cum_t[:, h : h + 1] - cum[h : h + 1, :], -1e30)
            parts.append(nn((jnp.exp(spread) * inner).astype(bf16), x))
        if h1 > h0:
            half = iota((tokens, end - begin), 1) < size
            intra[:, begin:end] = jnp.where(half, parts[0], parts[1])
        else:
            intra[:, begin:end] = parts[0]
        weighted = (x.astype(f32) * by_head(tail, span)).astype(bf16)
        pay[0:state, begin:end] = tn(b_part, weighted).astype(bf16)
        whole = by_head(carry, span)
        high = whole.astype(bf16).astype(f32)
        at = place[:, : end - begin]
        pay[state : state + PAD, begin:end] = jnp.where(
            at == 0, high, jnp.where(at == 1, whole - high, 0.0)
        ).astype(bf16)


def parts_of(pay):
    state = pay.shape[0] - PAD
    scale = pay[state : state + PAD, :].astype(f32)
    return pay[0:state, :].astype(f32), scale[0:1, :] + scale[1:2, :]


def store_pay(out, total, scale):
    state = total.shape[0]
    out[0:state, :] = total.astype(bf16)
    high = scale.astype(bf16).astype(f32)
    at = iota((PAD, total.shape[1]), 0)
    out[state : state + PAD, :] = jnp.where(
        at == 0, high, jnp.where(at == 1, scale - high, 0.0)
    ).astype(bf16)


def step_body(first, late, pay, got, *refs):
    before, new_pay, new_before = (None,) + refs if first else refs
    state = pay.shape[0] - PAD
    mine, my_scale = parts_of(pay)
    other, other_scale = parts_of(got)
    is_late = late[0] > 0
    total = jnp.where(is_late, my_scale * other + mine, other_scale * mine + other)
    store_pay(new_pay, total, my_scale * other_scale)
    if first:
        prefix, reach = jnp.where(is_late, other, 0.0), jnp.where(is_late, other_scale, 1.0)
    else:
        reach = before[state : state + 1, :]
        prefix = before[0:state, :] + jnp.where(is_late, reach, 0.0) * other
        reach = jnp.where(is_late, reach * other_scale, reach)
    new_before[0:state, :] = prefix
    new_before[state : state + 8, :] = jnp.broadcast_to(reach, (8, reach.shape[1]))


def last_step(late, before, got):
    state = got.shape[0] - PAD
    return before[0:state, :] + jnp.where(
        late[0] > 0, before[state : state + 1, :], 0.0
    ) * got[0:state, :].astype(f32)


def mix_body(late, before, got, intra, resid, proj, cum_t, sel, mixed, mixer, state_in, sent):
    heads, state = cum_t.shape[1], proj.shape[1] // 2
    width = intra.shape[1]
    entering = last_step(late, before, got).astype(bf16)
    state_in[...] = entering
    grown = jnp.exp(cum_t[...])
    carried = nn(proj[:, state:], entering)
    for span in spans(heads, width):
        begin, end = span[:2]
        out = intra[:, begin:end] + by_head(grown, span) * carried[:, begin:end]
        mixer[:, begin:end] = out
        mixed[:, begin:end] = (resid[:, begin:end].astype(f32) + out).astype(bf16)
    sent[...] = nn(sel[...], mixed[...]).astype(bf16)


def scan(axis, pay, reverse):
    count, me = lax.axis_size(axis), lax.axis_index(axis)
    size = pay.shape
    before_shape = struct((size[0] - PAD + 8, size[1]), f32)
    before, distance = None, 1
    while True:
        pairs = [(i, i ^ distance) for i in range(count)]
        got = lax.ppermute(pay, axis, pairs)
        bit = (me // distance) % 2
        late = (1 - bit if reverse else bit).astype(jnp.int32).reshape(1)
        if distance * 2 >= count:
            return late, before, got
        args = (late, pay, got) + (() if before is None else (before,))
        pay, before = call(
            functools.partial(step_body, before is None),
            [struct(size, bf16), before_shape],
            *args,
            smem=1,
        )
        distance *= 2


def gather_pieces(pieces, scratch):
    at = 0
    for piece in pieces:
        scratch[at : at + piece.shape[0], :] = piece[...]
        at += piece.shape[0]


def first_body(count, tiles, flip, *refs):
    pieces, weights, out, rows = refs[:count], refs[count:-2], refs[-2], refs[-1]
    j = pl.program_id(0)

    @pl.when(j == 0)
    def _():
        gather_pieces(pieces, rows)

    product = nt if flip else nn
    for k, weight in enumerate(weights):

        @pl.when((j >= k * tiles) & (j < (k + 1) * tiles))
        def _():
            out[...] = product(rows[...], weight[0]).astype(bf16)


def first_layer(pieces, weights, flip, tile=256):
    depth = pieces[0].shape[1]
    hidden = weights[0].shape[1] if flip else weights[0].shape[2]
    total = sum(p.shape[0] for p in pieces)
    tile = min(tile, hidden)
    tiles = hidden // tile
    specs = [pl.BlockSpec(p.shape, lambda j: (0, 0), pipeline_mode=pl.Buffered(1)) for p in pieces]
    for k in range(len(weights)):
        place = lambda j, k=k: jnp.clip(j - k * tiles, 0, tiles - 1)
        if flip:
            specs.append(pl.BlockSpec((1, tile, depth), lambda j, p=place: (0, p(j), 0)))
        else:
            specs.append(pl.BlockSpec((1, depth, tile), lambda j, p=place: (0, 0, p(j))))
    width = hidden * len(weights)
    return pl.pallas_call(
        functools.partial(first_body, len(pieces), tiles, flip),
        out_shape=struct((total, width), bf16),
        grid=(tiles * len(weights),),
        in_specs=specs,
        out_specs=pl.BlockSpec((total, tile), lambda j: (0, j)),
        scratch_shapes=[pltpu.VMEM((total, depth), bf16)],
        cost_estimate=pl.CostEstimate(
            flops=2 * total * depth * width,
            bytes_accessed=2 * (depth * width + total * (depth + width)),
            transcendentals=0,
        ),
    )(*pieces, *weights)


def reduced(parts, axis):
    count = lax.axis_size(axis)
    if count != 4:
        sums = [lax.psum(part, axis) for part in parts]
        return [(s, s) for s in sums]
    out = []
    for part in parts:
        inward = lax.ppermute(part, axis, [(0, 1), (3, 2)])
        half = part + inward
        across = lax.ppermute(half, axis, [(1, 2), (2, 1)])
        full = half + across
        outward = lax.ppermute(full, axis, [(1, 0), (2, 3)])
        out.append((full, outward))
    return out


def second_body(outer, gu_in, gu_out, bk_in, bk_out, w_gate, w_up, back, hidden, d_gate, d_up):
    j = pl.program_id(0)
    width = bk_in.shape[1]

    @pl.when(j == 0)
    def _():
        at_end = outer[0] > 0
        both = jnp.where(at_end, gu_out[...].astype(f32), gu_in[...].astype(f32))
        gate, up = both[:, :width], both[:, width:]
        grad = jnp.where(at_end, bk_out[...].astype(f32), bk_in[...].astype(f32))
        logistic = 1.0 / (1.0 + jnp.exp(-gate))
        active = gate * logistic
        slope = logistic * (1.0 + gate * (1.0 - logistic))
        hidden[...] = (active * up).astype(bf16)
        d_gate[...] = (grad * up * slope).astype(bf16)
        d_up[...] = (grad * active).astype(bf16)

    back[...] = (nt(d_gate[...], w_gate[0]) + nt(d_up[...], w_up[0])).astype(bf16)


def second_layer(outer, gu, bk, w_gate, w_up, tile=640):
    rows, width = bk[0].shape
    depth = w_gate.shape[1]
    tile = min(tile, depth)
    fixed = lambda a: pl.BlockSpec(a.shape, lambda j: (0, 0), pipeline_mode=pl.Buffered(1))
    return pl.pallas_call(
        second_body,
        out_shape=[struct((rows, depth), bf16), struct((rows, width), bf16)],
        grid=(pl.cdiv(depth, tile),),
        in_specs=[pl.BlockSpec(memory_space=pltpu.SMEM)]
        + [fixed(gu[0]), fixed(gu[1]), fixed(bk[0]), fixed(bk[1])]
        + [pl.BlockSpec((1, tile, width), lambda j: (0, j, 0))] * 2,
        out_specs=[
            pl.BlockSpec((rows, tile), lambda j: (0, j)),
            pl.BlockSpec((rows, width), lambda j: (0, 0)),
        ],
        scratch_shapes=[pltpu.VMEM((rows, width), bf16)] * 2,
        cost_estimate=pl.CostEstimate(
            flops=4 * rows * depth * width,
            bytes_accessed=4 * depth * width,
            transcendentals=rows * width,
        ),
    )(outer, *gu, *bk, w_gate, w_up)


def combine(sel_hi, sel_lo, pieces, rows):
    gather_pieces(pieces, rows)
    return tn(sel_hi[...], rows[...]) + tn(sel_lo[...], rows[...])


def final_body(count, sel_hi, sel_lo, mixed, *refs):
    pieces, out, rows = refs[:count], refs[count], refs[count + 1]
    out[...] = (mixed[...].astype(f32) + combine(sel_hi, sel_lo, pieces, rows)).astype(bf16)


def grad_body(count, sel_hi, sel_lo, cot, proj, cum_t, pay_in, *refs):
    pieces, (grad, pay, rows) = refs[:count], refs[count:]
    heads, state = cum_t.shape[1], proj.shape[1] // 2
    width = cot.shape[1]
    grad[...] = (cot[...].astype(f32) + combine(sel_hi, sel_lo, pieces, rows)).astype(bf16)
    grown = jnp.exp(cum_t[...])
    for span in spans(heads, width):
        begin, end = span[:2]
        scaled = (by_head(grown, span) * grad[:, begin:end].astype(f32)).astype(bf16)
        pay[0:state, begin:end] = tn(proj[:, state:], scaled).astype(bf16)
    pay[state : state + PAD, :] = pay_in[state : state + PAD, :]


def local_body(inputs, grad, proj, cum, cum_t, state_in, dx, d_c, d_b):
    tokens, width = inputs.shape
    heads, state = cum.shape[0], proj.shape[1] // 2
    b_part, c_part = proj[:, :state], proj[:, state:]
    inner = nt(b_part, c_part)
    source, later = iota((tokens, tokens), 0), iota((tokens, tokens), 1)
    causal = later >= source
    grown = jnp.exp(cum_t[...])
    d_inner = jnp.zeros((tokens, tokens), f32)
    d_c_sum = jnp.zeros((tokens, state), f32)
    for span in spans(heads, width):
        begin, end, h0, h1, size = span
        x, g = inputs[:, begin:end], grad[:, begin:end]
        half = iota((tokens, end - begin), 1) < size
        parts = []
        for h in (h0, h1)[: 1 + (h1 > h0)]:
            spread = jnp.where(causal, cum[h : h + 1, :] - cum_t[:, h : h + 1], -1e30)
            kernel = jnp.exp(spread)
            parts.append(nn((kernel * inner).astype(bf16), g))
            own = x
            if h1 > h0:
                own = jnp.where(half if h == h0 else ~half, x.astype(f32), 0.0).astype(bf16)
            d_inner = d_inner + kernel * nt(own, g)
        dx[:, begin:end] = jnp.where(half, parts[0], parts[-1])
        scaled = (by_head(grown, span) * g.astype(f32)).astype(bf16)
        d_c_sum = d_c_sum + nt(scaled, state_in[:, begin:end])
    d_inner = d_inner.astype(bf16)
    d_c[...] = (d_c_sum + tn(d_inner, b_part)).astype(bf16)
    d_b[...] = nn(d_inner, c_part)


def end_body(
    late, before, got, inputs, grad, mixer, proj, cum_t, dx, d_b, d_c, state_in, pay_in,
    d_input, d_proj, d_decay, change,
):
    tokens, width = inputs.shape
    heads, state = cum_t.shape[1], proj.shape[1] // 2
    leaving = last_step(late, before, got)
    rounded = leaving.astype(bf16)
    b_part = proj[:, :state]
    local, scale = parts_of(pay_in)
    both = leaving * (scale * state_in[...].astype(f32) + local)
    at_end = jnp.sum(both, axis=0, keepdims=True)
    tail = jnp.exp(cum_t[tokens - 1 : tokens, :] - cum_t[...])
    d_b_sum = d_b[...]
    for span in spans(heads, width):
        begin, end = span[:2]
        fading = by_head(tail, span)
        x = inputs[:, begin:end].astype(f32)
        total = dx[:, begin:end] + fading * nn(b_part, rounded[:, begin:end])
        d_input[:, begin:end] = total.astype(bf16)
        d_b_sum = d_b_sum + nt((x * fading).astype(bf16), rounded[:, begin:end])
        moved = grad[:, begin:end].astype(f32) * mixer[:, begin:end] - x * total
        final = iota((tokens, end - begin), 0) == tokens - 1
        change[:, begin:end] = moved + jnp.where(final, at_end[:, begin:end], 0.0)
    d_proj[:, :state] = d_b_sum.astype(bf16)
    d_proj[:, state:] = d_c[...]
    size = width // heads
    row, col = iota((heads, width), 0), iota((heads, width), 1)
    member = ((col >= row * size) & (col < (row + 1) * size)).astype(f32).astype(bf16)
    per_head = sum(nt(member, piece) for piece in split3(change[...]))
    reach = (iota((tokens, tokens), 0) >= iota((tokens, tokens), 1)).astype(f32)
    d_decay[...] = lax.dot_general(
        per_head, reach, (((1,), (0,)), ((), ())), precision=exact, preferred_element_type=f32
    )


def swap(blocks, axis, direct):
    count = lax.axis_size(axis)
    if direct:
        out = [None] * count
        out[0] = blocks[0]
        order = sorted(range(1, count), key=lambda j: -bin(j >> 1).count("1"))
        for j in order:
            out[j] = lax.ppermute(blocks[j], axis, [(i, i ^ j) for i in range(count)])
        return out
    whole = lax.all_to_all(jnp.stack(blocks), axis, split_axis=0, concat_axis=0, tiled=True)
    return [whole[j] for j in range(count)]


def cut(array, count):
    size = array.shape[0] // count
    return [array[j * size : (j + 1) * size] for j in range(count)]


def shards(
    resid, ssm_input, bc_proj, log_decay, experts_idx, route_weight, w_gate, w_up, w_down, cotangent
):
    tokens, width = resid.shape
    heads, state = log_decay.shape[0], bc_proj.shape[1] // 2
    ctx, rows_of = lax.axis_size("ctx"), lax.axis_index("ctx")
    experts = w_gate.shape[0] * ctx
    capacity = 3 * tokens // experts
    slots = capacity * experts
    hidden_width = w_gate.shape[2]
    direct = ctx <= 8 and ctx & (ctx - 1) == 0
    me = (rows_of if direct else rows_of * 0).astype(jnp.int32).reshape(1)
    spot = lax.axis_index("exp")
    outer = ((spot == 0) | (spot == lax.axis_size("exp") - 1)).astype(jnp.int32).reshape(1)
    block = jnp.asarray(np.arange(slots)[:, None] // capacity, jnp.int32)
    rank_of = jnp.asarray(np.arange(slots)[:, None] % capacity, f32)

    intra, pay, cum, cum_t = call(
        forward_body,
        [
            struct((tokens, width), f32),
            struct((state + PAD, width), bf16),
            struct((heads, tokens), f32),
            struct((tokens, heads), f32),
        ],
        ssm_input,
        bc_proj,
        log_decay,
    )
    sel, sel_hi, sel_lo, sent_cot = call(
        route_body,
        [struct((slots, tokens), bf16)] * 3 + [struct((slots, width), bf16)],
        me,
        experts_idx,
        route_weight,
        block,
        rank_of,
        cotangent,
        smem=1,
    )
    got_cot = swap(cut(sent_cot, ctx), "ctx", direct)
    late, before, got = scan("ctx", pay, False)
    mixed, mixer, state_in, sent_mixed = call(
        mix_body,
        [
            struct((tokens, width), bf16),
            struct((tokens, width), f32),
            struct((state, width), bf16),
            struct((slots, width), bf16),
        ],
        late,
        before,
        got,
        intra,
        resid,
        bc_proj,
        cum_t,
        sel,
        smem=1,
    )
    got_mixed = swap(cut(sent_mixed, ctx), "ctx", direct)
    half = ctx // 2
    chunks = [range(0, half), range(half, ctx)] if direct else [range(ctx)]
    bk_parts = [first_layer([got_cot[j] for j in c], [w_down], True) for c in chunks]
    bk = reduced(bk_parts, "exp")
    gu_parts = [first_layer([got_mixed[j] for j in c], [w_gate, w_up], False) for c in chunks]
    gu = reduced(gu_parts, "exp")
    back, out = [None] * ctx, [None] * ctx
    for n, c in enumerate(chunks):
        d_rows, hidden = second_layer(outer, gu[n], bk[n], w_gate, w_up)
        out_rows = nn(hidden, w_down[0]).astype(bf16)
        for j, d_block, o_block in zip(c, cut(d_rows, len(c)), cut(out_rows, len(c))):
            back[j], out[j] = d_block, o_block
    ret_back = swap(back, "ctx", direct)
    ret_out = swap(out, "ctx", direct)
    gathered = pltpu.VMEM((slots, width), bf16)
    d_resid, pay_back = call(
        functools.partial(grad_body, ctx),
        [struct((tokens, width), bf16), struct((state + PAD, width), bf16)],
        sel_hi,
        sel_lo,
        cotangent,
        bc_proj,
        cum_t,
        pay,
        *ret_back,
        scratch=[gathered],
    )
    late, before, got = scan("ctx", pay_back, True)
    dx, d_c, d_b = call(
        local_body,
        [struct((tokens, width), f32), struct((tokens, state), bf16), struct((tokens, state), f32)],
        ssm_input,
        d_resid,
        bc_proj,
        cum,
        cum_t,
        state_in,
    )
    (final,) = call(
        functools.partial(final_body, ctx),
        [struct((tokens, width), bf16)],
        sel_hi,
        sel_lo,
        mixed,
        *ret_out,
        scratch=[gathered],
    )
    d_input, d_proj, d_decay = call(
        end_body,
        [
            struct((tokens, width), bf16),
            struct((tokens, 2 * state), bf16),
            struct((heads, tokens), f32),
        ],
        late,
        before,
        got,
        ssm_input,
        d_resid,
        mixer,
        bc_proj,
        cum_t,
        dx,
        d_b,
        d_c,
        state_in,
        pay,
        smem=1,
        scratch=[pltpu.VMEM((tokens, width), f32)],
    )
    return final, d_resid, d_input, d_proj, d_decay


def solution(mesh):
    in_specs = (
        P("ctx", "exp"),
        P("ctx", "exp"),
        P("ctx", "exp"),
        P("exp", "ctx"),
        P("ctx", None),
        P("ctx", None),
        P("ctx", "exp", None),
        P("ctx", "exp", None),
        P("ctx", None, "exp"),
        P("ctx", "exp"),
    )
    out_specs = (
        P("ctx", "exp"),
        P("ctx", "exp"),
        P("ctx", "exp"),
        P("ctx", "exp"),
        P("exp", "ctx"),
    )
    return jax.shard_map(shards, mesh=mesh, in_specs=in_specs, out_specs=out_specs, check_vma=False)
```
